32 devices in a mesh: grp: 2 (over x), gy: 4 (over z), gz: 4 (over y, core).
Axes of the slice: x: 2, y: 2, z: 4, core: 2. Of those that a mesh axis runs over, the one named last changes fastest.
Arguments:
- vorticity: float32 [2, 3, 256, 256, 256], P('grp', None, 'gz', 'gy'), may hold values from -6 to 6
- wind: float32 [2, 3], P('grp'), may hold values from 0.5 to 1.2
Outputs:
- new_vorticity: float32 [2, 3, 256, 256, 256], P('grp', None, 'gz', 'gy')
- velocity: float32 [2, 3, 256, 256, 256], P('grp', None, 'gz', 'gy')
The draws below stay inside these ranges and needn't reach their ends.
All inputs are finite; a program needn't handle non-finite values.
Results may differ from the reference program's by a relative error of at most 0.0003.
Values sent between devices are 32-bit elements; how exact they have to be, the bound alone decides.
A program may use at most 192 MiB of HBM per device.

```python
import math
import jax
import jax.numpy as jnp

NX = 256
NY = 256
NZ = 256


def draw_vorticity(key, part):
    shape = (2, 3, NZ, NY, NX)
    first = jax.random.fold_in(key, 0)
    return jnp.clip(jax.random.normal(first, shape, jnp.float32), -6.0, 6.0)


def shard_levels(key, shape, cuts, smallest, largest):
    def one(position, parts):
        steps = jax.random.uniform(jax.random.fold_in(jax.random.fold_in(key, 6), position), (parts,), jnp.float32, smallest / len(cuts), largest / len(cuts))
        return jnp.repeat(jnp.exp(steps), shape[position] // parts).reshape((-1,) + (1,) * (len(shape) - position - 1))

    gain = one(*cuts[0])
    for cut in cuts[1:]:
        gain = gain * one(*cut)
    return gain


def setup_inputs(seed: int = 0) -> dict:
    key_of = jax.random.split(jax.random.key(seed), 3)
    vorticity = draw_vorticity(jax.random.fold_in(key_of[2], 71), 0)
    wind = jnp.clip(0.5 + 0.70000005 * jax.random.uniform(key_of[1], (2, 3), jnp.float32) ** shard_levels(key_of[1], (2, 3), ((0, 2),), -0.2, 0.2), 0.5, 1.2)
    return dict(vorticity=vorticity, wind=wind)


TIME_STEP = 0.4


def kernel_weight(offset):
    mag = jnp.abs(offset)
    inner = 1.0 - 2.5 * mag * mag + 1.5 * mag * mag * mag
    outer = 0.5 * (2.0 - mag) * (2.0 - mag) * (1.0 - mag)
    return jnp.where(mag < 1.0, inner, jnp.where(mag < 2.0, outer, 0.0 * mag))


def wave_numbers(count):
    index = jnp.arange(count, dtype=jnp.int32)
    signed = jnp.where(index < count // 2, index, index - count)
    return signed.astype(jnp.float32) * (2.0 * math.pi / count)


def velocity_of(field, drift):
    spectrum = jnp.fft.fftn(field, axes=(1, 2, 3))
    wave_z = wave_numbers(NZ)[:, None, None]
    wave_y = wave_numbers(NY)[None, :, None]
    wave_x = wave_numbers(NX)[None, None, :]
    squared = wave_x * wave_x + wave_y * wave_y + wave_z * wave_z
    inverse = jnp.where(squared > 0, 1.0 / jnp.where(squared > 0, squared, 1.0), 0.0 * squared)
    stream = spectrum * inverse
    cross_x = wave_y * stream[2] - wave_z * stream[1]
    cross_y = wave_z * stream[0] - wave_x * stream[2]
    cross_z = wave_x * stream[1] - wave_y * stream[0]
    result = jnp.real(jnp.fft.ifftn(1j * jnp.stack([cross_x, cross_y, cross_z]), axes=(1, 2, 3)))
    return result + drift[:, None, None, None]


def central(values, axis):
    return (jnp.roll(values, -1, axis) - jnp.roll(values, 1, axis)) * 0.5


def stretch(field, speed, grad_x):
    grad_y = central(speed, 2)
    grad_z = central(speed, 1)
    return field + TIME_STEP * (field[0:1] * grad_x + field[1:2] * grad_y + field[2:3] * grad_z)


def remesh_periodic(values, shift, axis):
    total = jnp.zeros_like(values)
    for offset in range(-2, 3):
        total = total + jnp.roll(values, offset, axis) * kernel_weight(offset - jnp.roll(shift, offset, axis))
    return total


def remesh_inflow(values, shift, ghost_values, ghost_shift):
    q_ext = jnp.concatenate([ghost_values, values, jnp.zeros_like(values[..., :2])], -1)
    d_ext = jnp.concatenate([ghost_shift, shift, jnp.zeros_like(shift[..., :2])], -1)
    total = jnp.zeros_like(values)
    for offset in range(-2, 3):
        start = 2 - offset
        total = total + q_ext[..., start:start + NX] * kernel_weight(offset - d_ext[..., start:start + NX])
    return total


def reference(vorticity, wind):
    speed_pre = velocity_of(vorticity[0], wind[0])
    speed_wake = velocity_of(vorticity[1], wind[1])
    strength_pre = stretch(vorticity[0], speed_pre, central(speed_pre, 3))
    extended = jnp.concatenate([speed_pre[..., NX - 1:], speed_wake, speed_wake[..., NX - 1:]], -1)
    grad_wake = (extended[..., 2:] - extended[..., :-2]) * 0.5
    strength_wake = stretch(vorticity[1], speed_wake, grad_wake)
    moved_pre = remesh_periodic(strength_pre, TIME_STEP * speed_pre[0:1], 3)
    moved_wake = remesh_inflow(strength_wake, TIME_STEP * speed_wake[0:1], strength_pre[..., NX - 2:], TIME_STEP * speed_pre[0:1][..., NX - 2:])
    outputs = []
    for moved, speed in ((moved_pre, speed_pre), (moved_wake, speed_wake)):
        lateral = remesh_periodic(moved, TIME_STEP * speed[1:2], 2)
        outputs.append(remesh_periodic(lateral, TIME_STEP * speed[2:3], 1))
    return jnp.stack(outputs), jnp.stack([speed_pre, speed_wake])
```

```python
import math

import jax
import jax.numpy as jnp
import numpy as np
from jax import lax
from jax.sharding import PartitionSpec as P

TIME_STEP = 0.4
HIGH = lax.Precision.HIGH


def shifted(value, axis, steps):
    count = lax.axis_size(axis)
    initial, last = (max(0, -steps), min(count, count - steps))
    return lax.ppermute(value, axis, [(source, source + steps) for source in range(initial, last)])


def extended_2(cells, sides, width):
    for axis, dim in sides:
        count = lax.axis_size(axis)
        head = lax.slice_in_dim(cells, 0, width, axis=dim)
        tail = lax.slice_in_dim(cells, cells.shape[dim] - width, cells.shape[dim], axis=dim)
        cells = jnp.concatenate(
            [
                lax.ppermute(tail, axis, [(i, (i + 1) % count) for i in range(count)]),
                cells,
                lax.ppermute(head, axis, [((i + 1) % count, i) for i in range(count)]),
            ],
            axis=dim,
        )
    return cells


def kernel_weight(offset):
    mag = jnp.abs(offset)
    inner = 1.0 - 2.5 * mag * mag + 1.5 * mag * mag * mag
    outer = 0.5 * (2.0 - mag) * (2.0 - mag) * (1.0 - mag)
    return jnp.where(mag < 1.0, inner, jnp.where(mag < 2.0, outer, 0.0 * mag))


def wave_numbers(index, count):
    signed = jnp.where(index < count // 2, index, index - count)
    return signed.astype(jnp.float32) * (2.0 * math.pi / count)


def odd_numbers(index, count):
    signed = jnp.where(index < count // 2, index, index - count)
    signed = jnp.where(index == count // 2, 0 * index, signed)
    return signed.astype(jnp.float32) * (2.0 * math.pi / count)


def curl_of(stream, wave_x, wave_y, wave_z):
    cross_x = wave_y * stream[2] - wave_z * stream[1]
    cross_y = wave_z * stream[0] - wave_x * stream[2]
    cross_z = wave_x * stream[1] - wave_y * stream[0]
    return jnp.stack([cross_x, cross_y, cross_z])


def reversed_lines(values):
    return jnp.roll(jnp.flip(values, (1, 2)), 1, (1, 2))


def curled_pair(real_in, imag_in, scaling, wave_y, wave_z):
    stream_real = real_in * scaling
    stream_imag = imag_in * scaling
    return (-curl_of(stream_imag, 0.0, wave_y, wave_z), curl_of(stream_real, 0.0, wave_y, wave_z))


def exchanged(pieces, axis):
    count = lax.axis_size(axis)
    received = [pieces[0]]
    for step in range(1, count):
        pairs = [(i, (i + step) % count) for i in range(count)]
        received.append(lax.ppermute(pieces[step], axis, pairs))
    return received


def relative(table, dim, axis, sign):
    count = lax.axis_size(axis)
    table = jnp.asarray(table, jnp.float32)
    steps = jnp.arange(count, dtype=jnp.int32)
    order = (lax.axis_index(axis) + sign * steps) % count
    return jnp.take(table, order, axis=dim)


def angles(count):
    positions = np.arange(count)
    product = positions[:, None] * positions[None, :] % count
    angle = product * (2.0 * np.pi / count)
    return (np.cos(angle), np.sin(angle))


def complex_table(count, inverse):
    cosine, sine = angles(count)
    if inverse:
        cosine, sine = (cosine / count, -sine / count)
    rows_real = np.stack([cosine, -sine], 1)
    rows_imag = np.stack([sine, cosine], 1)
    return np.stack([rows_real, rows_imag], 0)


def dot(letters, values, table):
    return jnp.einsum(letters, values, jnp.asarray(table, jnp.float32), precision=HIGH)


def body(vorticity, wind):
    is_wake = lax.axis_index("grp") == 1
    field = vorticity[0]
    drift = wind[0]
    count_x = field.shape[3]
    half_x = count_x // 2
    size_gy = lax.axis_size("gy")
    size_gz = lax.axis_size("gz")
    local_y = field.shape[2]
    count_y = local_y * size_gy
    count_z = field.shape[1] * size_gz
    cosine_x, sine_x = angles(count_x)
    alternate = 1.0 - 2.0 * (np.arange(count_x) % 2)
    forward_cos = cosine_x[:, :half_x]
    forward_sin = np.concatenate([alternate[:, None], -sine_x[:, 1:half_x]], 1)
    cosine_z, sine_z = angles(count_z)
    table_y = complex_table(count_y, False)
    table_y = table_y.reshape(2, size_gy, local_y, 2 * count_y)
    table_y = table_y.transpose(1, 0, 2, 3).reshape(2 * count_y, 2 * count_y)
    owner = lax.axis_index("gy") * size_gz + lax.axis_index("gz")
    share_x = half_x // (size_gy * size_gz)
    local_z = field.shape[1]
    split_x = (count_x, size_gy, size_gz, share_x)
    forward_cos = relative(forward_cos.reshape(split_x), 2, "gz", 1).reshape(count_x, half_x)
    forward_sin = relative(forward_sin.reshape(split_x), 2, "gz", 1).reshape(count_x, half_x)
    split_z = (size_gz, local_z, count_z)
    whole_z = (count_z, count_z)
    forward_z = [relative(t.reshape(split_z), 0, "gz", -1).reshape(whole_z) for t in (cosine_z, sine_z)]
    parts = []
    for comp in range(3):
        lines = jnp.concatenate(
            [
                dot("zyx,xk->kzy", field[comp], forward_cos),
                dot("zyx,xk->kzy", field[comp], forward_sin),
            ],
            2,
        )
        lines = lax.all_to_all(lines, "gy", split_axis=0, concat_axis=2, tiled=True)
        lines = dot("kzl,ln->kzn", lines, table_y)
        pieces = [
            lines[step * share_x : (step + 1) * share_x] for step in range(size_gz)
        ]
        lines = jnp.concatenate(exchanged(pieces, "gz"), 1)
        real_in, imag_in = (lines[..., :count_y], lines[..., count_y:])
        parts.append(
            (
                dot("kzy,zq->kqy", real_in, forward_z[0])
                + dot("kzy,zq->kqy", imag_in, forward_z[1]),
                dot("kzy,zq->kqy", imag_in, forward_z[0])
                - dot("kzy,zq->kqy", real_in, forward_z[1]),
            )
        )
    spectrum = jnp.stack([pair[0] for pair in parts] + [pair[1] for pair in parts])
    local_x = spectrum.shape[1]
    global_x = owner * local_x + jnp.arange(local_x, dtype=jnp.int32)
    index_z = jnp.arange(count_z, dtype=jnp.int32)
    index_y = jnp.arange(count_y, dtype=jnp.int32)
    wave_x = wave_numbers(global_x, count_x)[:, None, None]
    wave_z = wave_numbers(index_z, count_z)[None, :, None]
    wave_y = wave_numbers(index_y, count_y)[None, None, :]
    squared = wave_x * wave_x + wave_y * wave_y + wave_z * wave_z
    inverse = jnp.where(squared > 0, 1.0 / jnp.where(squared > 0, squared, 1.0), 0.0 * squared)
    curl_z = odd_numbers(index_z, count_z)[None, :, None]
    curl_y = odd_numbers(index_y, count_y)[None, None, :]
    stream_real = spectrum[:3] * inverse
    stream_imag = spectrum[3:] * inverse
    curled = jnp.concatenate(
        [
            -curl_of(stream_imag, wave_x, curl_y, curl_z),
            curl_of(stream_real, wave_x, curl_y, curl_z),
        ],
        0,
    )
    packed_plane = spectrum[:, 0]
    plain_real = packed_plane[:3]
    plain_imag = packed_plane[3:]
    mirror_real = reversed_lines(plain_real)
    mirror_imag = reversed_lines(plain_imag)
    base_real = 0.5 * (plain_real + mirror_real)
    base_imag = 0.5 * (plain_imag - mirror_imag)
    top_real = 0.5 * (plain_imag + mirror_imag)
    top_imag = -0.5 * (plain_real - mirror_real)
    plane_squared = wave_z[0] * wave_z[0] + wave_y[0] * wave_y[0]
    base_scale = jnp.where(
        plane_squared > 0,
        1.0 / jnp.where(plane_squared > 0, plane_squared, 1.0),
        0.0 * plane_squared,
    )
    top_scale = 1.0 / (plane_squared + math.pi * math.pi)
    base_vr, base_vi = curled_pair(base_real, base_imag, base_scale, curl_y[0], curl_z[0])
    top_vr, top_vi = curled_pair(top_real, top_imag, top_scale, curl_y[0], curl_z[0])
    rebuilt = jnp.concatenate([base_vr - top_vi, base_vi + top_vr], 0)
    chosen = jnp.where(global_x[0] == 0, rebuilt, curled[:, 0])
    curled = jnp.concatenate([chosen[:, None], curled[:, 1:]], 1)
    back_cos = np.concatenate([cosine_x[:1], 2.0 * cosine_x[1:half_x]], 0) / count_x
    back_sin = np.concatenate([-alternate[None, :], 2.0 * sine_x[1:half_x]], 0) / -count_x
    split_x = (size_gy, size_gz, share_x, count_x)
    back_cos = relative(back_cos.reshape(split_x), 1, "gz", -1).reshape(half_x, count_x)
    back_sin = relative(back_sin.reshape(split_x), 1, "gz", -1).reshape(half_x, count_x)
    split_z = (count_z, size_gz, local_z)
    cosine_z, sine_z = [
        relative(t.reshape(split_z) / count_z, 1, "gz", 1).reshape(whole_z)
        for t in (cosine_z, sine_z)
    ]
    table_y = complex_table(count_y, True)
    table_y = table_y.reshape(2 * count_y, 2, size_gy, local_y)
    table_y = table_y.transpose(2, 0, 1, 3).reshape(size_gy, 2 * count_y, 2 * local_y)
    speeds = []
    for comp in range(3):
        real_in, imag_in = (curled[comp], curled[comp + 3])
        lines = jnp.concatenate(
            [
                dot("kqy,qz->kzy", real_in, cosine_z) - dot("kqy,qz->kzy", imag_in, sine_z),
                dot("kqy,qz->kzy", imag_in, cosine_z) + dot("kqy,qz->kzy", real_in, sine_z),
            ],
            2,
        )
        pieces = [
            lines[:, step * local_z : (step + 1) * local_z] for step in range(size_gz)
        ]
        lines = jnp.concatenate(exchanged(pieces, "gz"), 0)
        lines = jnp.concatenate(
            [dot("kzn,nl->kzl", lines, table_y[side]) for side in range(size_gy)], 0
        )
        lines = lax.all_to_all(lines, "gy", split_axis=0, concat_axis=0, tiled=True)
        speeds.append(
            dot("kzy,kx->zyx", lines[..., :local_y], back_cos)
            + dot("kzy,kx->zyx", lines[..., local_y:], back_sin)
            + drift[comp]
        )
    velocity = jnp.stack(speeds)
    planes = shifted(velocity[..., count_x - 2 :], "grp", 1)
    rimmed = extended_2(velocity, (("gz", 1), ("gy", 2)), 1)
    grad_z = (rimmed[:, 2:, 1:-1, :] - rimmed[:, :-2, 1:-1, :]) * 0.5
    grad_y = (rimmed[:, 1:-1, 2:, :] - rimmed[:, 1:-1, :-2, :]) * 0.5
    left_side = jnp.where(is_wake, planes[..., 1:], velocity[..., count_x - 1 :])
    right_side = jnp.where(is_wake, velocity[..., count_x - 1 :], velocity[..., :1])
    extended = jnp.concatenate([left_side, velocity, right_side], -1)
    grad_x = (extended[..., 2:] - extended[..., :-2]) * 0.5
    strength = field + TIME_STEP * (field[0:1] * grad_x + field[1:2] * grad_y + field[2:3] * grad_z)
    ghost = shifted(strength[..., count_x - 2 :], "grp", 1)
    shift_x = TIME_STEP * velocity[0]
    left_q = jnp.where(is_wake, ghost, strength[..., count_x - 2 :])
    left_d = jnp.where(is_wake, TIME_STEP * planes[0], shift_x[..., count_x - 2 :])
    right_q = jnp.where(is_wake, 0.0, strength[..., :2])
    right_d = jnp.where(is_wake, 0.0, shift_x[..., :2])
    q_ext = jnp.concatenate([left_q, strength, right_q], -1)
    d_ext = jnp.concatenate([left_d, shift_x, right_d], -1)
    moved = jnp.zeros_like(strength)
    for offset in range(-2, 3):
        start = 2 - offset
        moved = moved + q_ext[..., start : start + count_x] * kernel_weight(
            offset - d_ext[..., start : start + count_x]
        )
    packed = jnp.concatenate([moved, TIME_STEP * velocity[1:2]], 0)
    rim_rows = extended_2(packed, (("gy", 2),), 2)
    width_y = moved.shape[2]
    lateral = jnp.zeros_like(moved)
    for offset in range(-2, 3):
        start = 2 - offset
        lateral = lateral + rim_rows[:3, :, start : start + width_y, :] * kernel_weight(
            offset - rim_rows[3:4, :, start : start + width_y, :]
        )
    packed = jnp.concatenate([lateral, TIME_STEP * velocity[2:3]], 0)
    rim_cols = extended_2(packed, (("gz", 1),), 2)
    width_z = moved.shape[1]
    result = jnp.zeros_like(moved)
    for offset in range(-2, 3):
        start = 2 - offset
        result = result + rim_cols[:3, start : start + width_z, :, :] * kernel_weight(
            offset - rim_cols[3:4, start : start + width_z, :, :]
        )
    return (result[None], velocity[None])


def solution(mesh):
    return jax.shard_map(
        body,
        mesh=mesh,
        in_specs=(P("grp", None, "gz", "gy", None), P("grp", None)),
        out_specs=(P("grp", None, "gz", "gy", None), P("grp", None, "gz", "gy", None)),
        check_vma=False,
    )
```
